256 devices in a mesh: group: 4 (over z_hi, core), leaf: 64 (over y, z_lo, x).
Axes of the slice: x: 4, y: 4, z: 8 (z_hi: 2, z_lo: 4; z = z_hi * 4 + z_lo), core: 2. Of those that a mesh axis runs over, the one named last changes fastest.
Arguments:
- top_modes: bfloat16 [1024, 512], P('group'), may hold values from -6 to 6
- low_modes: bfloat16 [16384, 512], P(('group', 'leaf')), may hold values from -6 to 6
- anc_top: int32 [256, 8], P(('group', 'leaf')), may hold values from 0 to 15, all different within a row
- anc_low: int32 [256, 24], P(('group', 'leaf')), may hold values from 0 to 63, all different within a row
- coupling: bfloat16 [393216, 2048], P(('group', 'leaf')), may hold values from -0.125 to 0.125
- leaf_mass: bfloat16 [393216, 1536], P(('group', 'leaf')), may hold values from -0.15625 to 0.15625
- leaf_modes: bfloat16 [393216, 128], P(('group', 'leaf')), may hold values from -0.5 to 0.5
- leaf_coef: bfloat16 [32768, 512], P(('group', 'leaf')), may hold values from -6 to 6
- kinv_top: float32 [1024, 64], P('group'), may hold values from -0.0625 to 0.0625
- kinv_low: float32 [16384, 64], P(('group', 'leaf')), may hold values from -0.15625 to 0.15625
Outputs:
- new_top: float32 [1024, 512], P('group')
- new_low: float32 [16384, 512], P(('group', 'leaf'))
- leaf_proj: bfloat16 [32768, 512], P(('group', 'leaf'))
The draws below stay inside these ranges and needn't reach their ends.
Inputs may be any that keep to these rules, and one draw needn't show every extreme that they name: `anc_top`: each row names 8 different top separator blocks. `anc_low`: each row names 24 different leaf indices of the leaf's own subtree.
All inputs are finite; a program needn't handle non-finite values.
Results may differ from the reference program's by a relative error of at most 0.0057.
Values may be sent and summed in bfloat16 or wider, within the bound.
A program may use at most 128 MiB of HBM per device.

```python
import jax
import jax.numpy as jnp
from jax import lax

M = 512
SR = 64
ANC_TOP = 8
KL = 128
NL = 1536
ANC_LOW = 24
SW = 2048
TOPS = 16
LEAVES = 256
N_GROUP = 4
N_LEAF = 64


def shard_levels(own_key, shape, split, least, high):
    loudness, own = 1.0, jax.random.fold_in(own_key, 6)
    for dim, blocks in split:
        steps = jnp.exp(jax.random.uniform(jax.random.fold_in(own, dim), (blocks,), jnp.float32, least / len(split), high / len(split)))
        loudness = loudness * jnp.repeat(steps, shape[dim] // blocks).reshape([-1 if axis == dim else 1 for axis in range(len(shape))])
    return loudness


def distinct(own_key, rows, amount, top, lift):
    order = jax.random.permutation(jax.random.fold_in(own_key, 1), amount)
    favour = order
    for power in range(3):
        favour = favour * favour // amount
    favour = favour * lift // amount
    chance = jax.random.randint(jax.random.fold_in(own_key, 2), (rows, amount), 0, 4096) + favour
    fixed_rows = jax.random.permutation(jax.random.fold_in(own_key, 3), rows)[jnp.arange(amount) % rows]
    chance = jnp.where(jnp.arange(rows)[:, None] == fixed_rows[None, :], 1 << 14, chance)
    priority = chance * amount + jnp.arange(amount)
    return lax.top_k(priority.astype(jnp.int32), top)[1].astype(jnp.int32)


def noise(stream_key, shape, width, bound, split=(), kind=jnp.bfloat16):
    values = jax.random.normal(stream_key, shape, jnp.float32) * width
    if len(split) > 0:
        values = shard_levels(stream_key, shape, split, -0.22, 0.18) * values
    return jnp.clip(values, min=-bound, max=bound).astype(kind)


def setup_inputs(seed: int = 0) -> dict:
    keys = jax.random.split(jax.random.key(seed), 11)
    top_modes = noise(keys[0], (TOPS * SR, M), 1.0, 6.0, ((0, 4),))
    low_modes = noise(keys[1], (LEAVES * SR, M), 1.0, 6.0, ((0, 256),))
    anc_top = distinct(keys[2], LEAVES, TOPS, ANC_TOP, 0)
    anc_low = distinct(keys[3], LEAVES, N_LEAF, ANC_LOW, 0)
    coupling = noise(keys[4], (LEAVES * NL, SW), SW ** -0.5, 0.125, ((0, 256),))
    leaf_mass = noise(keys[5], (LEAVES * NL, NL), NL ** -0.5, 0.15625, ((0, 256),))
    leaf_modes = noise(keys[6], (LEAVES * NL, KL), KL ** -0.5, 0.5, ((0, 256),))
    leaf_coef = noise(keys[7], (LEAVES * KL, M), 1.0, 6.0, ((0, 256),))
    kinv_top = noise(keys[8], (TOPS * SR, SR), (SR * LEAVES * ANC_TOP // TOPS) ** -0.5, 0.0625, ((0, 4),), jnp.float32)
    kinv_low = noise(keys[9], (LEAVES * SR, SR), (SR * ANC_LOW) ** -0.5, 0.15625, ((0, 256),), jnp.float32)
    return dict(top_modes=top_modes, low_modes=low_modes, anc_top=anc_top, anc_low=anc_low, coupling=coupling, leaf_mass=leaf_mass, leaf_modes=leaf_modes, leaf_coef=leaf_coef, kinv_top=kinv_top, kinv_low=kinv_low)


def reference(top_modes, low_modes, anc_top, anc_low, coupling, leaf_mass, leaf_modes, leaf_coef, kinv_top, kinv_low):
    top_blocks = top_modes.reshape(TOPS, SR, M)
    low_blocks = low_modes.reshape(N_GROUP, N_LEAF, SR, M)

    def one_leaf(totals, leaf_index):
        top_loads, low_loads = totals
        group_index = leaf_index // N_LEAF
        top_sel = top_blocks[anc_top[leaf_index]]
        low_sel = low_blocks[group_index][anc_low[leaf_index]]
        stacked = jnp.concatenate([top_sel, low_sel], axis=0).reshape(SW, M)
        coupler = lax.dynamic_slice_in_dim(coupling, leaf_index * NL, NL, 0)
        mass_block = lax.dynamic_slice_in_dim(leaf_mass, leaf_index * NL, NL, 0)
        basis = lax.dynamic_slice_in_dim(leaf_modes, leaf_index * NL, NL, 0)
        coeffs = lax.dynamic_slice_in_dim(leaf_coef, leaf_index * KL, KL, 0)
        shapes = (jnp.dot(basis, coeffs, preferred_element_type=jnp.float32)
                  - jnp.dot(coupler, stacked, preferred_element_type=jnp.float32)).astype(jnp.bfloat16)
        weighted = jnp.dot(mass_block, shapes, preferred_element_type=jnp.float32).astype(jnp.bfloat16)
        loads = jnp.dot(coupler.T, weighted, preferred_element_type=jnp.float32)
        projected = jnp.dot(basis.T, weighted, preferred_element_type=jnp.float32).astype(jnp.bfloat16)
        top_loads = top_loads.at[anc_top[leaf_index]].add(loads[:ANC_TOP * SR].reshape(ANC_TOP, SR, M))
        low_loads = low_loads.at[group_index, anc_low[leaf_index]].add(loads[ANC_TOP * SR:].reshape(ANC_LOW, SR, M))
        return (top_loads, low_loads), projected

    leaf_ids = jnp.arange(N_GROUP * N_LEAF, dtype=jnp.int32)
    start_totals = (jnp.zeros((TOPS, SR, M), jnp.float32), jnp.zeros((N_GROUP, N_LEAF, SR, M), jnp.float32))
    (top_loads, low_loads), projected = lax.scan(one_leaf, start_totals, leaf_ids)
    new_top = jnp.einsum("brs,bsm->brm", kinv_top.reshape(TOPS, SR, SR), top_loads,
                         precision=lax.Precision.HIGHEST).reshape(TOPS * SR, M)
    new_low = jnp.einsum("brs,bsm->brm", kinv_low.reshape(N_GROUP * N_LEAF, SR, SR),
                         low_loads.reshape(N_GROUP * N_LEAF, SR, M),
                         precision=lax.Precision.HIGHEST).reshape(N_GROUP * N_LEAF * SR, M)
    leaf_proj = projected.reshape(N_GROUP * N_LEAF * KL, M)
    return (new_top, new_low, leaf_proj)
```

```python
import functools

import jax
import jax.numpy as jnp
from jax import lax
from jax.experimental import pallas as pl
from jax.experimental.pallas import tpu as pltpu
from jax.sharding import PartitionSpec as P

MESH = pl.DeviceIdType.MESH
F32 = jnp.float32
BF16 = jnp.bfloat16


class Comm:
    def __init__(self, send_sem, recv_sem):
        self.send_sem, self.recv_sem = send_sem, recv_sem
        self.count = 0
        self.sent = []

    def ids(self, amount):
        first = self.count
        self.count += amount
        return list(range(first, first + amount))

    def copy(self, m, src, dst, dev):
        return pltpu.make_async_remote_copy(
            src_ref=src,
            dst_ref=dst,
            send_sem=self.send_sem.at[m],
            recv_sem=self.recv_sem.at[m],
            device_id=dev,
            device_id_type=MESH,
        )

    def send(self, m, src, dst, dev):
        c = self.copy(m, src, dst, dev)
        c.start()
        self.sent.append(c)

    def recv(self, m, dst, dev):
        self.copy(m, dst, dst, dev).wait_recv()

    def finish(self):
        for c in self.sent:
            c.wait_send()


def gather_steps(comm, buf, own, q, p, z, qdev, pdev, zdev):
    mz = comm.ids(3)
    mp = comm.ids(4)
    mq = comm.ids(16)
    for d in (1, 2, 3):
        comm.send(mz[d - 1], own, buf.at[q, p, z], zdev((z + d) % 4))
    yield
    for d in (1, 2, 3):
        comm.recv(mz[d - 1], buf.at[q, p, (z + 4 - d) % 4], zdev((z + d) % 4))
    up, down, far = (p + 1) % 4, (p + 3) % 4, (p + 2) % 4
    qup, qdown, qfar = (q + 1) % 4, (q + 3) % 4, (q + 2) % 4

    def row(j, r):
        comm.send(mq[4 * j], buf.at[q, r], buf.at[q, r], qdev(qup))
        comm.send(mq[4 * j + 1], buf.at[q, r], buf.at[q, r], qdev(qdown))

    def pass_on(j, r):
        comm.recv(mq[4 * j], buf.at[qdown, r], qdev(qup))
        comm.send(mq[4 * j + 2], buf.at[qdown, r, pl.ds(0, 2)], buf.at[qdown, r, pl.ds(0, 2)], qdev(qup))
        comm.recv(mq[4 * j + 1], buf.at[qup, r], qdev(qdown))
        comm.send(mq[4 * j + 3], buf.at[qup, r, pl.ds(2, 2)], buf.at[qup, r, pl.ds(2, 2)], qdev(qdown))

    comm.send(mp[0], buf.at[q, p], buf.at[q, p], pdev(up))
    comm.send(mp[1], buf.at[q, p], buf.at[q, p], pdev(down))
    row(0, p)
    yield
    comm.recv(mp[0], buf.at[q, down], pdev(up))
    comm.send(mp[2], buf.at[q, down, pl.ds(0, 2)], buf.at[q, down, pl.ds(0, 2)], pdev(up))
    comm.recv(mp[1], buf.at[q, up], pdev(down))
    comm.send(mp[3], buf.at[q, up, pl.ds(2, 2)], buf.at[q, up, pl.ds(2, 2)], pdev(down))
    row(1, down)
    row(2, up)
    yield
    pass_on(0, p)
    yield
    comm.recv(mp[2], buf.at[q, far, pl.ds(0, 2)], pdev(up))
    comm.recv(mp[3], buf.at[q, far, pl.ds(2, 2)], pdev(down))
    row(3, far)
    yield
    pass_on(1, down)
    yield
    pass_on(2, up)
    yield
    pass_on(3, far)
    yield
    for j, r in enumerate((p, down, up, far)):
        comm.recv(mq[4 * j + 2], buf.at[qfar, r, pl.ds(0, 2)], qdev(qup))
        comm.recv(mq[4 * j + 3], buf.at[qfar, r, pl.ds(2, 2)], qdev(qdown))


def add_into(dst, *srcs):
    total = dst[...].astype(F32)
    for s in srcs:
        total = total + s[...].astype(F32)
    dst[...] = total.astype(dst.dtype)


def scatter_steps(comm, s, r1a, r1b, r2a, r2b, rp1, rp2a, rp2b, rz, out, q, p, z, qdev, pdev, zdev):
    m1 = comm.ids(8)
    m2 = comm.ids(8)
    mp1 = comm.ids(2)
    mp2 = comm.ids(2)
    mz = comm.ids(3)
    up, down, far = (p + 1) % 4, (p + 3) % 4, (p + 2) % 4
    qup, qdown, qfar = (q + 1) % 4, (q + 3) % 4, (q + 2) % 4
    lo, hi = pl.ds(0, 2), pl.ds(2, 2)
    order = (far, up, down, p)
    for j, r in enumerate(order):
        comm.send(m1[2 * j], s.at[qfar, r, lo], r1a.at[r], qdev(qup))
        comm.send(m1[2 * j + 1], s.at[qfar, r, hi], r1b.at[r], qdev(qdown))
    yield
    for j, r in enumerate(order):
        comm.recv(m1[2 * j], r1a.at[r], qdev(qup))
        add_into(s.at[qup, r, lo], r1a.at[r])
        comm.send(m2[2 * j], s.at[qup, r], r2a.at[r], qdev(qup))
        comm.recv(m1[2 * j + 1], r1b.at[r], qdev(qdown))
        add_into(s.at[qdown, r, hi], r1b.at[r])
        comm.send(m2[2 * j + 1], s.at[qdown, r], r2b.at[r], qdev(qdown))
        yield
    for j, r in enumerate(order):
        comm.recv(m2[2 * j], r2a.at[r], qdev(qup))
        comm.recv(m2[2 * j + 1], r2b.at[r], qdev(qdown))
        add_into(s.at[q, r], r2a.at[r], r2b.at[r])
        if j == 0:
            comm.send(mp1[0], s.at[q, far, lo], rp1.at[0], pdev(up))
            comm.send(mp1[1], s.at[q, far, hi], rp1.at[1], pdev(down))
        if j == 1:
            comm.recv(mp1[0], rp1.at[0], pdev(up))
            add_into(s.at[q, up, lo], rp1.at[0])
            comm.send(mp2[0], s.at[q, up], rp2a, pdev(up))
        if j == 2:
            comm.recv(mp1[1], rp1.at[1], pdev(down))
            add_into(s.at[q, down, hi], rp1.at[1])
            comm.send(mp2[1], s.at[q, down], rp2b, pdev(down))
        yield
    comm.recv(mp2[0], rp2a, pdev(up))
    comm.recv(mp2[1], rp2b, pdev(down))
    add_into(s.at[q, p], rp2a, rp2b)
    for d in (1, 2, 3):
        comm.send(mz[d - 1], s.at[q, p, (z + d) % 4], rz.at[d - 1], zdev((z + d) % 4))
    yield
    for d in (1, 2, 3):
        comm.recv(mz[d - 1], rz.at[d - 1], zdev((z + d) % 4))
    total = s[q, p, z].astype(F32)
    for d in range(3):
        total = total + rz[d].astype(F32)
    out[...] = total


def run_together(*steps):
    live = list(steps)
    while live:
        for g in list(live):
            try:
                next(g)
            except StopIteration:
                live.remove(g)


def kernel(
    anc_top, anc_low, inv_top, inv_low,
    top_in, low_in, coef, kinv_top, kinv_low,
    coupling_hbm, mass_hbm, modes_hbm,
    new_top, new_low, proj,
    coupling, mass, modes, turned,
    low_a, low_b, tops, stacked, shapes, weighted,
    loads, top_loads, give, take,
    s_a, s_b, r1, r2, rp1, rp2, rz, sums,
    far_tile, gath_a, gath_b, full_top, full_low,
    local_sem, send_sem, recv_sem,
):
    leaf = lax.axis_index("leaf")
    group = lax.axis_index("group")
    y, z, x = leaf // 16, (leaf // 4) % 4, leaf % 4
    half, core = group // 2, group % 2
    mate = half * 2 + 1 - core
    across = (group + 2) % 4
    mate_across = (mate + 2) % 4

    def xdev(v):
        return {"leaf": y * 16 + z * 4 + v}

    def ydev(v):
        return {"leaf": v * 16 + z * 4 + x}

    def zdev(v):
        return {"leaf": y * 16 + v * 4 + x}

    mate_dev, across_dev = {"group": mate}, {"group": across}

    loading = [
        pltpu.make_async_copy(src, dst, local_sem.at[i])
        for i, (src, dst) in enumerate(((coupling_hbm, coupling), (modes_hbm, modes), (mass_hbm, mass)))
    ]
    for c in loading:
        c.start()

    barrier = pltpu.get_barrier_semaphore()
    peers = [xdev((x + d) % 4) for d in (1, 2, 3)] + [ydev((y + 1) % 4), ydev((y + 3) % 4)]
    peers += [zdev((z + d) % 4) for d in (1, 2, 3)] + [mate_dev, across_dev]
    for dev in peers:
        pl.semaphore_signal(barrier, inc=1, device_id=dev, device_id_type=MESH)
    low_a[x, y, z] = low_in[0]
    low_b[y, x, z] = low_in[1]
    tops[group] = top_in[...]
    pl.semaphore_wait(barrier, len(peers))

    comm = Comm(send_sem, recv_sem)
    steps_a = gather_steps(comm, low_a, low_in.at[0], x, y, z, xdev, ydev, zdev)
    steps_b = gather_steps(comm, low_b, low_in.at[1], y, x, z, ydev, xdev, zdev)
    next(steps_a)
    next(steps_b)

    mt = comm.ids(9)
    comm.send(mt[0], top_in, tops.at[group], mate_dev)
    comm.send(mt[1], top_in.at[x], tops.at[group, x], across_dev)

    def turn(i):
        @pl.loop(0, 8)
        def _(k):
            cols = pl.ds(pl.multiple_of(k * 256, 256), 256)
            turned[cols, pl.ds(i * 256, 256)] = coupling[pl.ds(i * 256, 256), cols].T

    def turn_modes():
        for i in range(6):
            turned[pl.ds(2048, 128), pl.ds(i * 256, 256)] = modes[pl.ds(i * 256, 256), :].T

    next(steps_a)
    next(steps_b)
    loading[0].wait()
    turn(0)
    next(steps_a)
    next(steps_b)
    turn(1)
    comm.recv(mt[1], tops.at[across, x], across_dev)
    for d in (1, 2, 3):
        comm.send(mt[1 + d], tops.at[across, x], tops.at[across, x], xdev((x + d) % 4))
    comm.send(mt[5], tops.at[across, x], tops.at[across, x], mate_dev)
    next(steps_a)
    next(steps_b)
    turn(2)
    next(steps_a)
    next(steps_b)
    turn(3)
    for d in (1, 2, 3):
        got = tops.at[across, (x + 4 - d) % 4]
        comm.recv(mt[1 + d], got, xdev((x + d) % 4))
        comm.send(mt[5 + d], got, got, mate_dev)
    next(steps_a)
    next(steps_b)
    turn(4)
    next(steps_a)
    next(steps_b)
    turn(5)
    loading[1].wait()
    turn_modes()
    next(steps_a)
    next(steps_b)
    comm.recv(mt[0], tops.at[mate], mate_dev)
    comm.recv(mt[5], tops.at[mate_across, x], mate_dev)
    for d in (1, 2, 3):
        comm.recv(mt[5 + d], tops.at[mate_across, (x + 4 - d) % 4], mate_dev)
    loading[2].wait()
    run_together(steps_a, steps_b)

    for j in range(8):
        b = anc_top[j]
        stacked[pl.ds(j * 64, 64), :] = tops[b // 4, b % 4]
    for j in range(24):
        k = anc_low[j]
        ky, kz, kx = k // 16, (k // 4) % 4, k % 4
        stacked[pl.ds(512 + j * 64, 32), :] = low_a[kx, ky, kz]
        stacked[pl.ds(512 + j * 64 + 32, 32), :] = low_b[ky, kx, kz]

    @pl.loop(0, 6)
    def _(i):
        rows = pl.ds(pl.multiple_of(i * 256, 256), 256)
        got = jnp.dot(modes[rows, :], coef[...], preferred_element_type=F32)
        got = got - jnp.dot(coupling[rows, :], stacked[...], preferred_element_type=F32)
        shapes[rows, :] = got.astype(BF16)

    @pl.loop(0, 6)
    def _(i):
        rows = pl.ds(pl.multiple_of(i * 256, 256), 256)
        weighted[rows, :] = jnp.dot(mass[rows, :], shapes[...], preferred_element_type=F32).astype(BF16)

    top_loads[0] = jnp.zeros(top_loads.shape[1:], BF16)
    loads[0] = jnp.zeros(loads.shape[1:], BF16)

    @pl.loop(0, 2)
    def _(i):
        rows = pl.ds(pl.multiple_of(i * 256, 256), 256)
        got = jnp.dot(turned[rows, :], weighted[...], preferred_element_type=F32).astype(BF16)
        for b in range(4):
            for r in range(4):
                for c in range(4):
                    top_loads[1 + i * 4 + b, r, c] = got[b * 64 + r * 16 : b * 64 + r * 16 + 16, c * 128 : c * 128 + 128]

    @pl.loop(0, 64)
    def _(t):
        b, r, c = t // 16, (t // 4) % 4, t % 4
        give[0, t] = top_loads[inv_top[4 * (1 - core) + b], r, c]
        give[1, t] = top_loads[inv_top[8 + 4 * (1 - core) + b], r, c]

    mx = comm.ids(2)
    comm.send(mx[0], give, take, mate_dev)

    @pl.loop(0, 6)
    def _(i):
        rows = pl.ds(pl.multiple_of(512 + i * 256, 256), 256)
        got = jnp.dot(turned[rows, :], weighted[...], preferred_element_type=F32).astype(BF16)
        for b in range(4):
            for r in range(4):
                for c in range(4):
                    loads[1 + i * 4 + b, r // 2, (r % 2) * 4 + c] = got[
                        b * 64 + r * 16 : b * 64 + r * 16 + 16, c * 128 : c * 128 + 128
                    ]

    comm.recv(mx[0], take, mate_dev)

    @pl.loop(0, 64)
    def _(t):
        a, b, c = t // 16, (t // 4) % 4, t % 4
        j = inv_low[b * 16 + c * 4 + a]
        s_a[a, b, c, pl.ds(0, 8)] = loads[j, 0]
        s_b[b, a, c, pl.ds(0, 8)] = loads[j, 1]
        mine = top_loads[inv_top[4 * core + a], b, c].astype(F32)
        s_a[a, b, c, 8] = (mine + take[0, t].astype(F32)).astype(BF16)
        mine = top_loads[inv_top[8 + 4 * core + a], b, c].astype(F32)
        s_b[b, a, c, 8] = (mine + take[1, t].astype(F32)).astype(BF16)

    sc_a = scatter_steps(
        comm, s_a, r1.at[0, 0], r1.at[0, 1], r2.at[0, 0], r2.at[0, 1], rp1.at[0], rp2.at[0, 0], rp2.at[0, 1],
        rz.at[0], sums.at[0], x, y, z, xdev, ydev, zdev,
    )
    sc_b = scatter_steps(
        comm, s_b, r1.at[1, 0], r1.at[1, 1], r2.at[1, 0], r2.at[1, 1], rp1.at[1], rp2.at[1, 0], rp2.at[1, 1],
        rz.at[1], sums.at[1], y, x, z, ydev, xdev, zdev,
    )
    next(sc_a)
    next(sc_b)
    proj[...] = jnp.dot(turned[pl.ds(2048, 128), :], weighted[...], preferred_element_type=F32).astype(BF16)
    run_together(sc_a, sc_b)

    comm.send(mx[1], sums.at[1 - half, 8], far_tile, across_dev)
    for h in range(2):
        for r in range(2):
            for c in range(4):
                full_low[h * 32 + r * 16 : h * 32 + r * 16 + 16, c * 128 : c * 128 + 128] = sums[h, r * 4 + c]
    new_low[...] = jnp.dot(kinv_low[...], full_low[...], preferred_element_type=F32, precision=lax.Precision.HIGHEST)
    comm.recv(mx[1], far_tile, across_dev)
    tile = sums[half, 8] + far_tile[...]
    gath_a[x, y, z] = tile[0:8, :]
    gath_b[y, x, z] = tile[8:16, :]
    run_together(
        gather_steps(comm, gath_a, gath_a.at[x, y, z], x, y, z, xdev, ydev, zdev),
        gather_steps(comm, gath_b, gath_b.at[y, x, z], y, x, z, ydev, xdev, zdev),
    )
    for b in range(4):
        for r in range(4):
            for c in range(4):
                cols = pl.ds(c * 128, 128)
                full_top[b, pl.ds(r * 16, 8), cols] = gath_a[b, r, c]
                full_top[b, pl.ds(r * 16 + 8, 8), cols] = gath_b[r, b, c]
    for b in range(4):
        rows = pl.ds(b * 64, 64)
        new_top[rows, :] = jnp.dot(
            kinv_top[rows, :], full_top[b], preferred_element_type=F32, precision=lax.Precision.HIGHEST
        )
    comm.finish()


def per_device(top_modes, low_modes, anc_top, anc_low, coupling, leaf_mass, leaf_modes, leaf_coef, kinv_top, kinv_low):
    inv_top = jnp.sum(
        jnp.where(anc_top == jnp.arange(16, dtype=jnp.int32)[:, None], jnp.arange(1, 9, dtype=jnp.int32)[None, :], 0), axis=1
    )
    inv_low = jnp.sum(
        jnp.where(anc_low == jnp.arange(64, dtype=jnp.int32)[:, None], jnp.arange(1, 25, dtype=jnp.int32)[None, :], 0), axis=1
    )
    smem = pl.BlockSpec(memory_space=pltpu.SMEM)
    vmem = pl.BlockSpec(memory_space=pltpu.VMEM)
    hbm = pl.BlockSpec(memory_space=pl.ANY)
    piece = (16, 128)
    messages = 46 + 9 + 2 + 46 + 46
    return pl.pallas_call(
        kernel,
        out_shape=(
            jax.ShapeDtypeStruct((256, 512), F32),
            jax.ShapeDtypeStruct((64, 512), F32),
            jax.ShapeDtypeStruct((128, 512), BF16),
        ),
        in_specs=[smem] * 4 + [vmem] * 5 + [hbm] * 3,
        out_specs=(vmem, vmem, vmem),
        scratch_shapes=[
            pltpu.VMEM((1536, 2048), BF16),
            pltpu.VMEM((1536, 1536), BF16),
            pltpu.VMEM((1536, 128), BF16),
            pltpu.VMEM((2176, 1536), BF16),
            pltpu.VMEM((4, 4, 4, 32, 512), BF16),
            pltpu.VMEM((4, 4, 4, 32, 512), BF16),
            pltpu.VMEM((4, 4, 64, 512), BF16),
            pltpu.VMEM((2048, 512), BF16),
            pltpu.VMEM((1536, 512), BF16),
            pltpu.VMEM((1536, 512), BF16),
            pltpu.VMEM((25, 2, 8) + piece, BF16),
            pltpu.VMEM((9, 4, 4) + piece, BF16),
            pltpu.VMEM((2, 64) + piece, BF16),
            pltpu.VMEM((2, 64) + piece, BF16),
            pltpu.VMEM((4, 4, 4, 9) + piece, BF16),
            pltpu.VMEM((4, 4, 4, 9) + piece, BF16),
            pltpu.VMEM((2, 2, 4, 2, 9) + piece, BF16),
            pltpu.VMEM((2, 2, 4, 4, 9) + piece, BF16),
            pltpu.VMEM((2, 2, 2, 9) + piece, BF16),
            pltpu.VMEM((2, 2, 4, 9) + piece, BF16),
            pltpu.VMEM((2, 3, 9) + piece, BF16),
            pltpu.VMEM((2, 9) + piece, F32),
            pltpu.VMEM(piece, F32),
            pltpu.VMEM((4, 4, 4, 8, 128), F32),
            pltpu.VMEM((4, 4, 4, 8, 128), F32),
            pltpu.VMEM((4, 64, 512), F32),
            pltpu.VMEM((64, 512), F32),
            pltpu.SemaphoreType.DMA((3,)),
            pltpu.SemaphoreType.DMA((messages,)),
            pltpu.SemaphoreType.DMA((messages,)),
        ],
        compiler_params=pltpu.CompilerParams(
            collective_id=0, has_side_effects=True, vmem_limit_bytes=63000 * 1024
        ),
    )(
        anc_top[0], anc_low[0], inv_top, inv_low,
        top_modes.reshape(4, 64, 512), low_modes.reshape(2, 32, 512), leaf_coef, kinv_top, kinv_low,
        coupling, leaf_mass, leaf_modes,
    )


def solution(mesh):
    both = P(("group", "leaf"), None)
    return jax.shard_map(
        per_device,
        mesh=mesh,
        in_specs=(P("group", None), both, both, both, both, both, both, both, P("group", None), both),
        out_specs=(P("group", None), both, both),
        check_vma=False,
    )
```

```python
import functools

import jax
import jax.numpy as jnp
from jax import lax
from jax.experimental import pallas as pl
from jax.experimental.pallas import tpu as pltpu
from jax.sharding import PartitionSpec as P

MESH = pl.DeviceIdType.MESH
F32 = jnp.float32
BF16 = jnp.bfloat16


GATHER_PLAN = "af0at1a2ta3bat4abt5abt6ab"
FIRST_PLAN = "vbvbvbvbvvvsj"
SECOND_PLAN = "wwsssswwwsqwsssu"
LAST_PLAN = "kpsuuuuqspuuqpuuuqpu"


class Comm:
    def __init__(self, send_sem, recv_sem):
        self.send_sem, self.recv_sem = send_sem, recv_sem
        self.count = 0
        self.sent = []

    def ids(self, amount):
        first = self.count
        self.count += amount
        return list(range(first, first + amount))

    def copy(self, m, src, dst, dev):
        return pltpu.make_async_remote_copy(
            src_ref=src,
            dst_ref=dst,
            send_sem=self.send_sem.at[m],
            recv_sem=self.recv_sem.at[m],
            device_id=dev,
            device_id_type=MESH,
        )

    def send(self, m, src, dst, dev):
        c = self.copy(m, src, dst, dev)
        c.start()
        self.sent.append(c)

    def recv(self, m, dst, dev):
        self.copy(m, dst, dst, dev).wait_recv()

    def finish(self):
        for c in self.sent:
            c.wait_send()


def gather_steps(comm, buf, own, q, p, z, qdev, pdev, zdev):
    mz = comm.ids(3)
    mp = comm.ids(4)
    mq = comm.ids(16)
    for d in (1, 2, 3):
        comm.send(mz[d - 1], own, buf.at[q, p, z], zdev((z + d) % 4))
    yield
    for d in (1, 2, 3):
        comm.recv(mz[d - 1], buf.at[q, p, (z + 4 - d) % 4], zdev((z + d) % 4))
    up, down, far = (p + 1) % 4, (p + 3) % 4, (p + 2) % 4
    qup, qdown, qfar = (q + 1) % 4, (q + 3) % 4, (q + 2) % 4

    def row(j, r):
        comm.send(mq[4 * j], buf.at[q, r], buf.at[q, r], qdev(qup))
        comm.send(mq[4 * j + 1], buf.at[q, r], buf.at[q, r], qdev(qdown))

    def pass_on(j, r):
        comm.recv(mq[4 * j], buf.at[qdown, r], qdev(qup))
        comm.send(mq[4 * j + 2], buf.at[qdown, r, pl.ds(0, 2)], buf.at[qdown, r, pl.ds(0, 2)], qdev(qup))
        comm.recv(mq[4 * j + 1], buf.at[qup, r], qdev(qdown))
        comm.send(mq[4 * j + 3], buf.at[qup, r, pl.ds(2, 2)], buf.at[qup, r, pl.ds(2, 2)], qdev(qdown))

    comm.send(mp[0], buf.at[q, p], buf.at[q, p], pdev(up))
    comm.send(mp[1], buf.at[q, p], buf.at[q, p], pdev(down))
    row(0, p)
    yield
    comm.recv(mp[0], buf.at[q, down], pdev(up))
    comm.send(mp[2], buf.at[q, down, pl.ds(0, 2)], buf.at[q, down, pl.ds(0, 2)], pdev(up))
    comm.recv(mp[1], buf.at[q, up], pdev(down))
    comm.send(mp[3], buf.at[q, up, pl.ds(2, 2)], buf.at[q, up, pl.ds(2, 2)], pdev(down))
    row(1, down)
    row(2, up)
    yield
    pass_on(0, p)
    yield
    comm.recv(mp[2], buf.at[q, far, pl.ds(0, 2)], pdev(up))
    comm.recv(mp[3], buf.at[q, far, pl.ds(2, 2)], pdev(down))
    row(3, far)
    yield
    pass_on(1, down)
    yield
    pass_on(2, up)
    yield
    pass_on(3, far)
    yield
    for j, r in enumerate((p, down, up, far)):
        comm.recv(mq[4 * j + 2], buf.at[qfar, r, pl.ds(0, 2)], qdev(qup))
        comm.recv(mq[4 * j + 3], buf.at[qfar, r, pl.ds(2, 2)], qdev(qdown))


def add_into(dst, *srcs):
    total = dst[...].astype(F32)
    for s in srcs:
        total = total + s[...].astype(F32)
    dst[...] = total.astype(dst.dtype)


def scatter_steps(comm, s, r1, r2, rp1, rp2, rz, out, q, p, z, qdev, pdev, zdev):
    m1 = comm.ids(8)
    m2 = comm.ids(8)
    mp1 = comm.ids(2)
    mp2 = comm.ids(2)
    mz = comm.ids(3)
    up, down, far = (p + 1) % 4, (p + 3) % 4, (p + 2) % 4
    qup, qdown, qfar = (q + 1) % 4, (q + 3) % 4, (q + 2) % 4
    lo, hi = pl.ds(0, 2), pl.ds(2, 2)
    order = (far, up, down, p)
    for j, r in enumerate(order):
        comm.send(m1[2 * j], s.at[qfar, r, lo], r1.at[0, r], qdev(qup))
        comm.send(m1[2 * j + 1], s.at[qfar, r, hi], r1.at[1, r], qdev(qdown))
    yield
    for j, r in enumerate(order):
        comm.recv(m1[2 * j], r1.at[0, r], qdev(qup))
        add_into(s.at[qup, r, lo], r1.at[0, r])
        comm.send(m2[2 * j], s.at[qup, r], r2.at[0, r], qdev(qup))
        comm.recv(m1[2 * j + 1], r1.at[1, r], qdev(qdown))
        add_into(s.at[qdown, r, hi], r1.at[1, r])
        comm.send(m2[2 * j + 1], s.at[qdown, r], r2.at[1, r], qdev(qdown))
        yield
    for j, r in enumerate(order):
        comm.recv(m2[2 * j], r2.at[0, r], qdev(qup))
        comm.recv(m2[2 * j + 1], r2.at[1, r], qdev(qdown))
        add_into(s.at[q, r], r2.at[0, r], r2.at[1, r])
        if j == 0:
            comm.send(mp1[0], s.at[q, far, lo], rp1.at[0], pdev(up))
            comm.send(mp1[1], s.at[q, far, hi], rp1.at[1], pdev(down))
        if j == 1:
            comm.recv(mp1[0], rp1.at[0], pdev(up))
            add_into(s.at[q, up, lo], rp1.at[0])
            comm.send(mp2[0], s.at[q, up], rp2.at[0], pdev(up))
        if j == 2:
            comm.recv(mp1[1], rp1.at[1], pdev(down))
            add_into(s.at[q, down, hi], rp1.at[1])
            comm.send(mp2[1], s.at[q, down], rp2.at[1], pdev(down))
        yield
    comm.recv(mp2[0], rp2.at[0], pdev(up))
    comm.recv(mp2[1], rp2.at[1], pdev(down))
    add_into(s.at[q, p], rp2.at[0], rp2.at[1])
    for d in (1, 2, 3):
        comm.send(mz[d - 1], s.at[q, p, (z + d) % 4], rz.at[d - 1], zdev((z + d) % 4))
    yield
    for d in (1, 2, 3):
        comm.recv(mz[d - 1], rz.at[d - 1], zdev((z + d) % 4))
    total = s[q, p, z].astype(F32)
    for d in range(3):
        total = total + rz[d].astype(F32)
    out[...] = total


def top_steps(comm, tops, group, mate, across, mate_across, x, y, z, xdev, ydev, zdev, mate_dev, across_dev):
    m_own = comm.ids(1)
    m_far = comm.ids(2)
    m_line = comm.ids(6)
    m_ring = comm.ids(8)
    m_mate = comm.ids(8)
    lines = ((0, x, xdev), (1, y, ydev))
    lo, hi = pl.ds(0, 2), pl.ds(2, 2)
    for h, v, _ in lines:
        got = tops.at[group, v, h, z]
        comm.send(m_far[h], got, got, across_dev)
    comm.send(m_own[0], tops.at[group], tops.at[group], mate_dev)
    yield
    for h, v, _ in lines:
        got = tops.at[across, v, h, z]
        comm.recv(m_far[h], got, across_dev)
        for d in (1, 2, 3):
            comm.send(m_line[3 * h + d - 1], got, got, zdev((z + d) % 4))
    yield
    for h, v, dev in lines:
        for d in (1, 2, 3):
            comm.recv(m_line[3 * h + d - 1], tops.at[across, v, h, (z + 4 - d) % 4], zdev((z + d) % 4))
        got = tops.at[across, v, h]
        comm.send(m_ring[4 * h], got, got, dev((v + 1) % 4))
        comm.send(m_ring[4 * h + 1], got, got, dev((v + 3) % 4))
        comm.send(m_mate[4 * h], got, got, mate_dev)
    yield
    for h, v, dev in lines:
        low, high = tops.at[across, (v + 3) % 4, h], tops.at[across, (v + 1) % 4, h]
        comm.recv(m_ring[4 * h], low, dev((v + 1) % 4))
        comm.send(m_ring[4 * h + 2], low.at[lo], low.at[lo], dev((v + 1) % 4))
        comm.send(m_mate[4 * h + 1], low, low, mate_dev)
        comm.recv(m_ring[4 * h + 1], high, dev((v + 3) % 4))
        comm.send(m_ring[4 * h + 3], high.at[hi], high.at[hi], dev((v + 3) % 4))
        comm.send(m_mate[4 * h + 2], high, high, mate_dev)
    yield
    for h, v, dev in lines:
        got = tops.at[across, (v + 2) % 4, h]
        comm.recv(m_ring[4 * h + 2], got.at[lo], dev((v + 1) % 4))
        comm.recv(m_ring[4 * h + 3], got.at[hi], dev((v + 3) % 4))
        comm.send(m_mate[4 * h + 3], got, got, mate_dev)
    yield
    comm.recv(m_own[0], tops.at[mate], mate_dev)
    for h, v, _ in lines:
        for i, w in enumerate((v, (v + 3) % 4, (v + 1) % 4, (v + 2) % 4)):
            comm.recv(m_mate[4 * h + i], tops.at[mate_across, w, h], mate_dev)


def advance(*steps):
    for g in steps:
        next(g, None)


def run_together(*steps):
    live = list(steps)
    while live:
        for g in list(live):
            try:
                next(g)
            except StopIteration:
                live.remove(g)


def kernel(
    anc_top, anc_low,
    top_hbm, low_hbm, coef_hbm, kinv_top_hbm, kinv_low_hbm, coupling_hbm, mass_hbm, modes_hbm,
    new_top, new_low, proj,
    coef, kinv_top, kinv_low, coupling, mass, modes, turned, kinv_turned,
    low_a0, low_a1, low_b0, low_b1, tops, stacked, shapes, weighted,
    loads, top_loads, give, take,
    s_low, r1, r2, rp1, rp2, rz, sums,
    s_top, tp, line_out, line_in, gath, full_top, full_low,
    inv_top, inv_low, local_sem, send_sem, recv_sem,
):
    low_a, low_b = (low_a0, low_a1), (low_b0, low_b1)
    leaf = lax.axis_index("leaf")
    group = lax.axis_index("group")
    y, z, x = leaf // 16, (leaf // 4) % 4, leaf % 4
    half, core = group // 2, group % 2
    mate = half * 2 + 1 - core
    across = (group + 2) % 4
    mate_across = (mate + 2) % 4

    def xdev(v):
        return {"leaf": y * 16 + z * 4 + v}

    def ydev(v):
        return {"leaf": v * 16 + z * 4 + x}

    def zdev(v):
        return {"leaf": y * 16 + v * 4 + x}

    def far_zdev(v):
        return {"group": across, "leaf": y * 16 + v * 4 + x}

    mate_dev, across_dev = {"group": mate}, {"group": across}
    lines = ((x, y, z, xdev, ydev, zdev), (y, x, z, ydev, xdev, zdev))

    barrier = pltpu.get_barrier_semaphore()
    peers = [
        {"leaf": (y + b) % 4 * 16 + z * 4 + (x + a) % 4} for a in range(4) for b in range(4) if a + b > 0
    ]
    peers += [zdev((z + d) % 4) for d in (1, 2, 3)] + [mate_dev] + [far_zdev((z + d) % 4) for d in range(4)]
    for dev in peers:
        pl.semaphore_signal(barrier, inc=1, device_id=dev, device_id_type=MESH)

    fetched = [
        (low_hbm.at[0, :, pl.ds(0, 256)], low_a[0].at[x, y, z]),
        (low_hbm.at[1, :, pl.ds(0, 256)], low_b[0].at[y, x, z]),
        (low_hbm.at[0, :, pl.ds(256, 256)], low_a[1].at[x, y, z]),
        (low_hbm.at[1, :, pl.ds(256, 256)], low_b[1].at[y, x, z]),
        *((top_hbm.at[:, :, :, pl.ds(128 * k, 128)], tops.at[group, :, :, k]) for k in range(4)),
        (coupling_hbm, coupling),
        (modes_hbm, modes),
        (coef_hbm, coef),
        (mass_hbm, mass),
        (kinv_top_hbm, kinv_turned),
        (kinv_low_hbm, kinv_low),
    ]
    fetch = [pltpu.make_async_copy(src, dst, local_sem.at[i]) for i, (src, dst) in enumerate(fetched)]
    for c in fetch:
        c.start()

    @pl.loop(0, 64)
    def _(k):
        found = jnp.int32(0)
        for j in range(24):
            found = jnp.where(anc_low[j] == k, jnp.int32(j + 1), found)
        inv_low[k] = found

    @pl.loop(0, 16)
    def _(k):
        found = jnp.int32(0)
        for j in range(8):
            found = jnp.where(anc_top[j] == k, jnp.int32(j + 1), found)
        inv_top[k] = found

    loads[0] = jnp.zeros(loads.shape[1:], BF16)
    for c in range(2):
        top_loads[c, 0] = jnp.zeros(top_loads.shape[2:], F32)
    for i in range(8):
        fetch[i].wait()
    pl.semaphore_wait(barrier, len(peers))

    comm = Comm(send_sem, recv_sem)
    ga = [gather_steps(comm, low_a[c], low_a[c].at[x, y, z], *lines[0]) for c in range(2)]
    gb = [gather_steps(comm, low_b[c], low_b[c].at[y, x, z], *lines[1]) for c in range(2)]
    gt = top_steps(
        comm, tops, group, mate, across, mate_across, x, y, z, xdev, ydev, zdev, mate_dev, across_dev
    )

    def turn(i):
        @pl.loop(0, 8)
        def _(k):
            cols = pl.ds(pl.multiple_of(k * 256, 256), 256)
            turned[cols, pl.ds(i * 256, 256)] = coupling[pl.ds(i * 256, 256), cols].T

    def turn_modes():
        for i in range(6):
            turned[pl.ds(2048, 128), pl.ds(i * 256, 256)] = modes[pl.ds(i * 256, 256), :].T
        kinv_top[...] = kinv_turned[...].T

    def compute_steps(c):
        cols = pl.ds(c * 256, 256)
        for j in range(8):
            b = anc_top[j]
            for h in range(2):
                for k in range(2):
                    part = tops[b // 4, b % 4, h, 2 * c + k]
                    stacked[pl.ds(j * 64 + h * 32, 32), pl.ds(128 * k, 128)] = part
        for j in range(24):
            k = anc_low[j]
            ky, kz, kx = k // 16, (k // 4) % 4, k % 4
            stacked[pl.ds(512 + j * 64, 32), :] = low_a[c][kx, ky, kz]
            stacked[pl.ds(512 + j * 64 + 32, 32), :] = low_b[c][ky, kx, kz]
        yield
        halves = (pl.ds(0, 768), pl.ds(768, 768))
        got = [jnp.dot(coupling[rows, :], stacked[...], preferred_element_type=F32) for rows in halves]
        more = [jnp.dot(modes[rows, :], coef[:, cols], preferred_element_type=F32) for rows in halves]
        for rows, g, m in zip(halves, got, more):
            shapes[rows, :] = (m - g).astype(BF16)
        yield
        got = [jnp.dot(mass[rows, :], shapes[...], preferred_element_type=F32) for rows in halves]
        for rows, g in zip(halves, got):
            weighted[rows, :] = g.astype(BF16)
        yield
        got = [jnp.dot(turned[pl.ds(256 * i, 256), :], weighted[...], preferred_element_type=F32) for i in range(2)]
        for b in range(8):
            for r in range(8):
                for t in range(2):
                    first = (b % 4) * 64 + r * 8
                    top_loads[c, 1 + b, r, t] = got[b // 4][first : first + 8, t * 128 : t * 128 + 128]

        @pl.loop(0, 64, unroll=4)
        def _(t):
            i, r, k = t // 16, (t // 2) % 8, t % 2
            one = top_loads[c, inv_top[4 * (1 - core) + i], r, k]
            two = top_loads[c, inv_top[8 + 4 * (1 - core) + i], r, k]
            give[c, t] = jnp.concatenate([one, two], axis=0).astype(BF16)

        comm.send(m_swap[c], give.at[c], take.at[c], mate_dev)
        yield
        got = [jnp.dot(turned[pl.ds(512 + 768 * i, 768), :], weighted[...], preferred_element_type=F32) for i in range(2)]
        for b in range(24):
            for h in range(2):
                for r in range(2):
                    for t in range(2):
                        first = (b % 12) * 64 + h * 32 + r * 16
                        part = got[b // 12][first : first + 16, t * 128 : t * 128 + 128]
                        loads[1 + b, h, r * 2 + t] = part.astype(BF16)
        yield

        @pl.loop(0, 64, unroll=4)
        def _(k):
            ky, kz, kx = k // 16, (k // 4) % 4, k % 4
            j = inv_low[k]
            s_low[c, 0, kx, ky, kz] = loads[j, 0]
            s_low[c, 1, ky, kx, kz] = loads[j, 1]

    def project(c):
        cols = pl.ds(c * 256, 256)
        proj[:, cols] = jnp.dot(turned[pl.ds(2048, 128), :], weighted[...], preferred_element_type=F32).astype(BF16)

    def top_path(c):
        q, p = lines[c][:2]
        m, m_line, m_back = comm.ids(15), comm.ids(7), comm.ids(15)
        s, pt, out, got, g = s_top.at[c], tp.at[c], line_out.at[c], line_in.at[c], gath.at[c]
        offsets = [(dq, dp) for dq in range(4) for dp in range(4) if dq + dp > 0]
        plane = sorted(offsets, key=lambda v: -(min(v[0], 4 - v[0]) + min(v[1], 4 - v[1])))

        def plane_dev(v, w):
            return {"leaf": w * 16 + z * 4 + v} if c == 0 else {"leaf": v * 16 + z * 4 + w}

        comm.recv(m_swap[c], take.at[c], mate_dev)

        @pl.loop(0, 64, unroll=4)
        def _(t):
            i, r, k = t // 16, (t // 2) % 8, t % 2
            one = top_loads[c, inv_top[4 * core + i], r, k]
            two = top_loads[c, inv_top[8 + 4 * core + i], r, k]
            mine = jnp.concatenate([one, two], axis=0) + take[c, t].astype(F32)
            s_top[c, t // 16, (t // 4) % 4, t % 4] = mine.astype(BF16)

        for i, (dq, dp) in enumerate(plane):
            to_q, to_p = (q + dq) % 4, (p + dp) % 4
            comm.send(m[i], s.at[to_q, to_p], pt.at[i], plane_dev(to_q, to_p))
        yield
        total = s_top[c, q, p].astype(F32)
        for i, (dq, dp) in enumerate(plane):
            comm.recv(m[i], pt.at[i], plane_dev((q + dq) % 4, (p + dp) % 4))
            total = total + tp[c, i].astype(F32)
        for h in range(2):
            for k in range(2):
                two = [total[2 * k + i, 8 * h : 8 * h + 8] for i in range(2)]
                line_out[c, h, k] = jnp.concatenate(two, axis=0).astype(BF16)
        for d in (1, 2, 3):
            comm.send(m_line[d - 1], out.at[half], got.at[d - 1], zdev((z + d) % 4))
        for d in range(4):
            comm.send(m_line[3 + d], out.at[1 - half], got.at[3 + d], far_zdev((z + d) % 4))
        yield
        total = line_out[c, half].astype(F32)
        for d in (1, 2, 3):
            comm.recv(m_line[d - 1], got.at[d - 1], zdev((z + d) % 4))
            total = total + line_in[c, d - 1].astype(F32)
        for d in range(4):
            comm.recv(m_line[3 + d], got.at[3 + d], far_zdev((z + d) % 4))
            total = total + line_in[c, 3 + d].astype(F32)
        gath[c, q, p] = total.astype(BF16)
        for i, (dq, dp) in enumerate(plane):
            comm.send(m_back[i], g.at[q, p], g.at[q, p], plane_dev((q + dq) % 4, (p + dp) % 4))
        yield
        for i, (dq, dp) in enumerate(plane):
            comm.recv(m_back[i], g.at[(q + 4 - dq) % 4, (p + 4 - dp) % 4], plane_dev((q + dq) % 4, (p + dp) % 4))
        for t in range(64):
            i, r, k = t // 16, (t // 2) % 8, t % 2
            part = gath[c, t // 16, (t // 4) % 4, (t % 4) // 2].astype(F32)[(t % 2) * 8 : (t % 2) * 8 + 8]
            full_top[i, pl.ds(r * 8, 8), pl.ds(c * 256 + k * 128, 128)] = part

    def scatter(c, h):
        return scatter_steps(
            comm, s_low.at[c, h], r1.at[c, h], r2.at[c, h], rp1.at[c, h], rp2.at[c, h], rz.at[c, h], sums.at[c, h],
            *lines[h],
        )

    m_swap = comm.ids(2)

    work = [compute_steps(0), compute_steps(1)]
    sc = [scatter(0, 0), scatter(0, 1), scatter(1, 0), scatter(1, 1)]
    path = [top_path(0), top_path(1)]

    def run_plan(plan):
        for step in plan:
            if step == "a":
                advance(ga[0], gb[0])
            elif step == "b":
                advance(ga[1], gb[1])
            elif step == "t":
                advance(gt)
            elif step in "vw":
                advance(work["vw".index(step)])
            elif step == "s":
                advance(sc[0], sc[1])
            elif step == "u":
                advance(sc[2], sc[3])
            elif step in "pq":
                advance(path["pq".index(step)])
            elif step in "jk":
                project("jk".index(step))
            elif step == "f":
                fetch[8].wait()
            elif step == "6":
                for i in range(9, len(fetch)):
                    fetch[i].wait()
                turn_modes()
            else:
                turn(int(step))

    run_plan(GATHER_PLAN)
    run_together(ga[0], gb[0], gt)
    run_plan(FIRST_PLAN)
    run_together(work[0], ga[1], gb[1])
    run_plan(SECOND_PLAN)
    run_together(work[1])
    run_plan(LAST_PLAN)
    run_together(path[1], sc[0], sc[1], sc[2], sc[3], path[0])

    for c in range(2):
        for h in range(2):
            for r in range(2):
                for t in range(2):
                    rows, cols = pl.ds(h * 32 + r * 16, 16), pl.ds(c * 256 + t * 128, 128)
                    full_low[rows, cols] = sums[c, h, r * 2 + t]
    new_low[...] = jnp.dot(kinv_low[...], full_low[...], preferred_element_type=F32, precision=lax.Precision.HIGHEST)
    for b in range(4):
        rows = pl.ds(b * 64, 64)
        new_top[rows, :] = jnp.dot(
            kinv_top[rows, :], full_top[b], preferred_element_type=F32, precision=lax.Precision.HIGHEST
        )
    comm.finish()


def per_device(top_modes, low_modes, anc_top, anc_low, coupling, leaf_mass, leaf_modes, leaf_coef, kinv_top, kinv_low):
    smem = pl.BlockSpec(memory_space=pltpu.SMEM)
    vmem = pl.BlockSpec(memory_space=pltpu.VMEM)
    hbm = pl.BlockSpec(memory_space=pl.ANY)
    tile, four = (16, 128), (4, 16, 128)
    messages = 4 * 23 + 25 + 4 * 23 + 2 * 37 + 2
    return pl.pallas_call(
        kernel,
        out_shape=(
            jax.ShapeDtypeStruct((256, 512), F32),
            jax.ShapeDtypeStruct((64, 512), F32),
            jax.ShapeDtypeStruct((128, 512), BF16),
        ),
        in_specs=[smem] * 2 + [hbm] * 8,
        out_specs=(vmem, vmem, vmem),
        scratch_shapes=[
            pltpu.VMEM((128, 512), BF16),
            pltpu.VMEM((256, 64), F32),
            pltpu.VMEM((64, 64), F32),
            pltpu.VMEM((1536, 2048), BF16),
            pltpu.VMEM((1536, 1536), BF16),
            pltpu.VMEM((1536, 128), BF16),
            pltpu.VMEM((2176, 1536), BF16),
            pltpu.VMEM((64, 256), F32),
            *([pltpu.VMEM((4, 4, 4, 32, 256), BF16)] * 4),
            pltpu.VMEM((4, 4, 2, 4, 32, 128), BF16),
            pltpu.VMEM((2048, 256), BF16),
            pltpu.VMEM((1536, 256), BF16),
            pltpu.VMEM((1536, 256), BF16),
            pltpu.VMEM((25, 2) + four, BF16),
            pltpu.VMEM((2, 9, 8, 2, 8, 128), F32),
            pltpu.VMEM((2, 64) + tile, BF16),
            pltpu.VMEM((2, 64) + tile, BF16),
            pltpu.VMEM((2, 2, 4, 4, 4) + four, BF16),
            pltpu.VMEM((2, 2, 2, 4, 2) + four, BF16),
            pltpu.VMEM((2, 2, 2, 4, 4) + four, BF16),
            pltpu.VMEM((2, 2, 2, 2) + four, BF16),
            pltpu.VMEM((2, 2, 2, 4) + four, BF16),
            pltpu.VMEM((2, 2, 3) + four, BF16),
            pltpu.VMEM((2, 2) + four, F32),
            pltpu.VMEM((2, 4, 4, 4) + tile, BF16),
            pltpu.VMEM((2, 15, 4) + tile, BF16),
            pltpu.VMEM((2, 2, 2) + tile, BF16),
            pltpu.VMEM((2, 7, 2) + tile, BF16),
            pltpu.VMEM((2, 4, 4, 2) + tile, BF16),
            pltpu.VMEM((4, 64, 512), F32),
            pltpu.VMEM((64, 512), F32),
            pltpu.SMEM((16,), jnp.int32),
            pltpu.SMEM((64,), jnp.int32),
            pltpu.SemaphoreType.DMA((14,)),
            pltpu.SemaphoreType.DMA((messages,)),
            pltpu.SemaphoreType.DMA((messages,)),
        ],
        compiler_params=pltpu.CompilerParams(
            collective_id=0, has_side_effects=True, vmem_limit_bytes=63000 * 1024
        ),
    )(
        anc_top[0], anc_low[0],
        top_modes.reshape(4, 2, 32, 512), low_modes.reshape(2, 32, 512), leaf_coef, kinv_top.T, kinv_low,
        coupling, leaf_mass, leaf_modes,
    )


def solution(mesh):
    both = P(("group", "leaf"), None)
    return jax.shard_map(
        per_device,
        mesh=mesh,
        in_specs=(P("group", None), both, both, both, both, both, both, both, P("group", None), both),
        out_specs=(P("group", None), both, both),
        check_vma=False,
    )
```

```python
import functools

import jax
import jax.numpy as jnp
from jax import lax
from jax.experimental import pallas as pl
from jax.experimental.pallas import tpu as pltpu
from jax.sharding import PartitionSpec as P

MESH = pl.DeviceIdType.MESH
F32 = jnp.float32
BF16 = jnp.bfloat16


GATHER_PLAN = "af0at1a2ta3bat4abt5abt6ab"
FIRST_PLAN = "vbvbvbvbvvvsj"
SECOND_PLAN = "wwsssswwwsqwsssu"
LAST_PLAN = "kpsuuuuqspuuqpuuuqpu"


class Comm:
    def __init__(self, send_sem, recv_sem):
        self.send_sem, self.recv_sem = send_sem, recv_sem
        self.count = 0
        self.sent = []

    def ids(self, amount):
        first = self.count
        self.count += amount
        return list(range(first, first + amount))

    def copy(self, m, src, dst, dev):
        return pltpu.make_async_remote_copy(
            src_ref=src,
            dst_ref=dst,
            send_sem=self.send_sem.at[m],
            recv_sem=self.recv_sem.at[m],
            device_id=dev,
            device_id_type=MESH,
        )

    def send(self, m, src, dst, dev):
        c = self.copy(m, src, dst, dev)
        c.start()
        self.sent.append(c)

    def recv(self, m, dst, dev):
        self.copy(m, dst, dst, dev).wait_recv()

    def finish(self):
        for c in self.sent:
            c.wait_send()


def gather_steps(comm, buf, own, q, p, z, qdev, pdev, zdev):
    mz = comm.ids(3)
    mp = comm.ids(4)
    mq = comm.ids(16)
    for d in (1, 2, 3):
        comm.send(mz[d - 1], own, buf.at[q, p, z], zdev((z + d) % 4))
    yield
    for d in (1, 2, 3):
        comm.recv(mz[d - 1], buf.at[q, p, (z + 4 - d) % 4], zdev((z + d) % 4))
    up, down, far = (p + 1) % 4, (p + 3) % 4, (p + 2) % 4
    qup, qdown, qfar = (q + 1) % 4, (q + 3) % 4, (q + 2) % 4

    def row(j, r):
        comm.send(mq[4 * j], buf.at[q, r], buf.at[q, r], qdev(qup))
        comm.send(mq[4 * j + 1], buf.at[q, r], buf.at[q, r], qdev(qdown))

    def pass_on(j, r):
        comm.recv(mq[4 * j], buf.at[qdown, r], qdev(qup))
        comm.send(mq[4 * j + 2], buf.at[qdown, r, pl.ds(0, 2)], buf.at[qdown, r, pl.ds(0, 2)], qdev(qup))
        comm.recv(mq[4 * j + 1], buf.at[qup, r], qdev(qdown))
        comm.send(mq[4 * j + 3], buf.at[qup, r, pl.ds(2, 2)], buf.at[qup, r, pl.ds(2, 2)], qdev(qdown))

    comm.send(mp[0], buf.at[q, p], buf.at[q, p], pdev(up))
    comm.send(mp[1], buf.at[q, p], buf.at[q, p], pdev(down))
    row(0, p)
    yield
    comm.recv(mp[0], buf.at[q, down], pdev(up))
    comm.send(mp[2], buf.at[q, down, pl.ds(0, 2)], buf.at[q, down, pl.ds(0, 2)], pdev(up))
    comm.recv(mp[1], buf.at[q, up], pdev(down))
    comm.send(mp[3], buf.at[q, up, pl.ds(2, 2)], buf.at[q, up, pl.ds(2, 2)], pdev(down))
    row(1, down)
    row(2, up)
    yield
    pass_on(0, p)
    yield
    comm.recv(mp[2], buf.at[q, far, pl.ds(0, 2)], pdev(up))
    comm.recv(mp[3], buf.at[q, far, pl.ds(2, 2)], pdev(down))
    row(3, far)
    yield
    pass_on(1, down)
    yield
    pass_on(2, up)
    yield
    pass_on(3, far)
    yield
    for j, r in enumerate((p, down, up, far)):
        comm.recv(mq[4 * j + 2], buf.at[qfar, r, pl.ds(0, 2)], qdev(qup))
        comm.recv(mq[4 * j + 3], buf.at[qfar, r, pl.ds(2, 2)], qdev(qdown))


def add_into(dst, *srcs):
    total = dst[...].astype(F32)
    for s in srcs:
        total = total + s[...].astype(F32)
    dst[...] = total.astype(dst.dtype)


def scatter_steps(comm, s, r1, r2, rp1, rp2, rz, out, q, p, z, qdev, pdev, zdev):
    m1 = comm.ids(8)
    m2 = comm.ids(8)
    mp1 = comm.ids(2)
    mp2 = comm.ids(2)
    mz = comm.ids(3)
    up, down, far = (p + 1) % 4, (p + 3) % 4, (p + 2) % 4
    qup, qdown, qfar = (q + 1) % 4, (q + 3) % 4, (q + 2) % 4
    lo, hi = pl.ds(0, 2), pl.ds(2, 2)
    order = (far, up, down, p)
    for j, r in enumerate(order):
        comm.send(m1[2 * j], s.at[qfar, r, lo], r1.at[0, r], qdev(qup))
        comm.send(m1[2 * j + 1], s.at[qfar, r, hi], r1.at[1, r], qdev(qdown))
    yield
    for j, r in enumerate(order):
        comm.recv(m1[2 * j], r1.at[0, r], qdev(qup))
        add_into(s.at[qup, r, lo], r1.at[0, r])
        comm.send(m2[2 * j], s.at[qup, r], r2.at[0, r], qdev(qup))
        comm.recv(m1[2 * j + 1], r1.at[1, r], qdev(qdown))
        add_into(s.at[qdown, r, hi], r1.at[1, r])
        comm.send(m2[2 * j + 1], s.at[qdown, r], r2.at[1, r], qdev(qdown))
        yield
    for j, r in enumerate(order):
        comm.recv(m2[2 * j], r2.at[0, r], qdev(qup))
        comm.recv(m2[2 * j + 1], r2.at[1, r], qdev(qdown))
        add_into(s.at[q, r], r2.at[0, r], r2.at[1, r])
        if j == 0:
            comm.send(mp1[0], s.at[q, far, lo], rp1.at[0], pdev(up))
            comm.send(mp1[1], s.at[q, far, hi], rp1.at[1], pdev(down))
        if j == 1:
            comm.recv(mp1[0], rp1.at[0], pdev(up))
            add_into(s.at[q, up, lo], rp1.at[0])
            comm.send(mp2[0], s.at[q, up], rp2.at[0], pdev(up))
        if j == 2:
            comm.recv(mp1[1], rp1.at[1], pdev(down))
            add_into(s.at[q, down, hi], rp1.at[1])
            comm.send(mp2[1], s.at[q, down], rp2.at[1], pdev(down))
        yield
    comm.recv(mp2[0], rp2.at[0], pdev(up))
    comm.recv(mp2[1], rp2.at[1], pdev(down))
    add_into(s.at[q, p], rp2.at[0], rp2.at[1])
    for d in (1, 2, 3):
        comm.send(mz[d - 1], s.at[q, p, (z + d) % 4], rz.at[d - 1], zdev((z + d) % 4))
    yield
    for d in (1, 2, 3):
        comm.recv(mz[d - 1], rz.at[d - 1], zdev((z + d) % 4))
    total = s[q, p, z].astype(F32)
    for d in range(3):
        total = total + rz[d].astype(F32)
    out[...] = total


def top_steps(comm, tops, group, mate, across, mate_across, x, y, z, xdev, ydev, zdev, mate_dev, across_dev):
    m_own = comm.ids(1)
    m_far = comm.ids(2)
    m_line = comm.ids(6)
    m_ring = comm.ids(8)
    m_mate = comm.ids(8)
    lines = ((0, x, xdev), (1, y, ydev))
    lo, hi = pl.ds(0, 2), pl.ds(2, 2)
    for h, v, _ in lines:
        got = tops.at[group, v, h, z]
        comm.send(m_far[h], got, got, across_dev)
    comm.send(m_own[0], tops.at[group], tops.at[group], mate_dev)
    yield
    for h, v, _ in lines:
        got = tops.at[across, v, h, z]
        comm.recv(m_far[h], got, across_dev)
        for d in (1, 2, 3):
            comm.send(m_line[3 * h + d - 1], got, got, zdev((z + d) % 4))
    yield
    for h, v, dev in lines:
        for d in (1, 2, 3):
            comm.recv(m_line[3 * h + d - 1], tops.at[across, v, h, (z + 4 - d) % 4], zdev((z + d) % 4))
        got = tops.at[across, v, h]
        comm.send(m_ring[4 * h], got, got, dev((v + 1) % 4))
        comm.send(m_ring[4 * h + 1], got, got, dev((v + 3) % 4))
        comm.send(m_mate[4 * h], got, got, mate_dev)
    yield
    for h, v, dev in lines:
        low, high = tops.at[across, (v + 3) % 4, h], tops.at[across, (v + 1) % 4, h]
        comm.recv(m_ring[4 * h], low, dev((v + 1) % 4))
        comm.send(m_ring[4 * h + 2], low.at[lo], low.at[lo], dev((v + 1) % 4))
        comm.send(m_mate[4 * h + 1], low, low, mate_dev)
        comm.recv(m_ring[4 * h + 1], high, dev((v + 3) % 4))
        comm.send(m_ring[4 * h + 3], high.at[hi], high.at[hi], dev((v + 3) % 4))
        comm.send(m_mate[4 * h + 2], high, high, mate_dev)
    yield
    for h, v, dev in lines:
        got = tops.at[across, (v + 2) % 4, h]
        comm.recv(m_ring[4 * h + 2], got.at[lo], dev((v + 1) % 4))
        comm.recv(m_ring[4 * h + 3], got.at[hi], dev((v + 3) % 4))
        comm.send(m_mate[4 * h + 3], got, got, mate_dev)
    yield
    comm.recv(m_own[0], tops.at[mate], mate_dev)
    for h, v, _ in lines:
        for i, w in enumerate((v, (v + 3) % 4, (v + 1) % 4, (v + 2) % 4)):
            comm.recv(m_mate[4 * h + i], tops.at[mate_across, w, h], mate_dev)


def advance(*steps):
    for g in steps:
        next(g, None)


def run_together(*steps):
    live = list(steps)
    while live:
        for g in list(live):
            try:
                next(g)
            except StopIteration:
                live.remove(g)


def kernel(
    anc_top, anc_low,
    top_hbm, low_hbm, coef_hbm, coupling_hbm, mass_hbm, modes_hbm,
    full_top, full_low, proj,
    coef, coupling, mass, modes, turned,
    low_a0, low_a1, low_b0, low_b1, tops, stacked, shapes, weighted,
    loads, top_loads, give, take,
    s_low, r1, r2, rp1, rp2, rz, sums,
    s_top, tp, line_out, line_in, gath,
    inv_top, inv_low, local_sem, send_sem, recv_sem,
):
    low_a, low_b = (low_a0, low_a1), (low_b0, low_b1)
    leaf = lax.axis_index("leaf")
    group = lax.axis_index("group")
    y, z, x = leaf // 16, (leaf // 4) % 4, leaf % 4
    half, core = group // 2, group % 2
    mate = half * 2 + 1 - core
    across = (group + 2) % 4
    mate_across = (mate + 2) % 4

    def xdev(v):
        return {"leaf": y * 16 + z * 4 + v}

    def ydev(v):
        return {"leaf": v * 16 + z * 4 + x}

    def zdev(v):
        return {"leaf": y * 16 + v * 4 + x}

    def far_zdev(v):
        return {"group": across, "leaf": y * 16 + v * 4 + x}

    mate_dev, across_dev = {"group": mate}, {"group": across}
    lines = ((x, y, z, xdev, ydev, zdev), (y, x, z, ydev, xdev, zdev))

    barrier = pltpu.get_barrier_semaphore()
    peers = [
        {"leaf": (y + b) % 4 * 16 + z * 4 + (x + a) % 4} for a in range(4) for b in range(4) if a + b > 0
    ]
    peers += [zdev((z + d) % 4) for d in (1, 2, 3)] + [mate_dev] + [far_zdev((z + d) % 4) for d in range(4)]
    for dev in peers:
        pl.semaphore_signal(barrier, inc=1, device_id=dev, device_id_type=MESH)

    fetched = [
        (low_hbm.at[0, :, pl.ds(0, 256)], low_a[0].at[x, y, z]),
        (low_hbm.at[1, :, pl.ds(0, 256)], low_b[0].at[y, x, z]),
        (low_hbm.at[0, :, pl.ds(256, 256)], low_a[1].at[x, y, z]),
        (low_hbm.at[1, :, pl.ds(256, 256)], low_b[1].at[y, x, z]),
        *((top_hbm.at[:, :, :, pl.ds(128 * k, 128)], tops.at[group, :, :, k]) for k in range(4)),
        (coupling_hbm, coupling),
        (modes_hbm, modes),
        (coef_hbm, coef),
        (mass_hbm, mass),
    ]
    fetch = [pltpu.make_async_copy(src, dst, local_sem.at[i]) for i, (src, dst) in enumerate(fetched)]
    for c in fetch:
        c.start()

    @pl.loop(0, 64)
    def _(k):
        found = jnp.int32(0)
        for j in range(24):
            found = jnp.where(anc_low[j] == k, jnp.int32(j + 1), found)
        inv_low[k] = found

    @pl.loop(0, 16)
    def _(k):
        found = jnp.int32(0)
        for j in range(8):
            found = jnp.where(anc_top[j] == k, jnp.int32(j + 1), found)
        inv_top[k] = found

    loads[0] = jnp.zeros(loads.shape[1:], BF16)
    for c in range(2):
        top_loads[c, 0] = jnp.zeros(top_loads.shape[2:], F32)
    for i in range(8):
        fetch[i].wait()
    pl.semaphore_wait(barrier, len(peers))

    comm = Comm(send_sem, recv_sem)
    ga = [gather_steps(comm, low_a[c], low_a[c].at[x, y, z], *lines[0]) for c in range(2)]
    gb = [gather_steps(comm, low_b[c], low_b[c].at[y, x, z], *lines[1]) for c in range(2)]
    gt = top_steps(
        comm, tops, group, mate, across, mate_across, x, y, z, xdev, ydev, zdev, mate_dev, across_dev
    )

    def turn(i):
        @pl.loop(0, 8)
        def _(k):
            cols = pl.ds(pl.multiple_of(k * 256, 256), 256)
            turned[cols, pl.ds(i * 256, 256)] = coupling[pl.ds(i * 256, 256), cols].T

    def turn_modes():
        for i in range(6):
            turned[pl.ds(2048, 128), pl.ds(i * 256, 256)] = modes[pl.ds(i * 256, 256), :].T

    def compute_steps(c):
        cols = pl.ds(c * 256, 256)
        for j in range(8):
            b = anc_top[j]
            for h in range(2):
                for k in range(2):
                    part = tops[b // 4, b % 4, h, 2 * c + k]
                    stacked[pl.ds(j * 64 + h * 32, 32), pl.ds(128 * k, 128)] = part
        for j in range(24):
            k = anc_low[j]
            ky, kz, kx = k // 16, (k // 4) % 4, k % 4
            stacked[pl.ds(512 + j * 64, 32), :] = low_a[c][kx, ky, kz]
            stacked[pl.ds(512 + j * 64 + 32, 32), :] = low_b[c][ky, kx, kz]
        yield
        halves = (pl.ds(0, 768), pl.ds(768, 768))
        got = [jnp.dot(coupling[rows, :], stacked[...], preferred_element_type=F32) for rows in halves]
        more = [jnp.dot(modes[rows, :], coef[:, cols], preferred_element_type=F32) for rows in halves]
        for rows, g, m in zip(halves, got, more):
            shapes[rows, :] = (m - g).astype(BF16)
        yield
        got = [jnp.dot(mass[rows, :], shapes[...], preferred_element_type=F32) for rows in halves]
        for rows, g in zip(halves, got):
            weighted[rows, :] = g.astype(BF16)
        yield
        got = [jnp.dot(turned[pl.ds(256 * i, 256), :], weighted[...], preferred_element_type=F32) for i in range(2)]
        for b in range(8):
            for r in range(8):
                for t in range(2):
                    first = (b % 4) * 64 + r * 8
                    top_loads[c, 1 + b, r, t] = got[b // 4][first : first + 8, t * 128 : t * 128 + 128]

        @pl.loop(0, 64, unroll=4)
        def _(t):
            i, r, k = t // 16, (t // 2) % 8, t % 2
            one = top_loads[c, inv_top[4 * (1 - core) + i], r, k]
            two = top_loads[c, inv_top[8 + 4 * (1 - core) + i], r, k]
            give[c, t] = jnp.concatenate([one, two], axis=0).astype(BF16)

        comm.send(m_swap[c], give.at[c], take.at[c], mate_dev)
        yield
        got = [jnp.dot(turned[pl.ds(512 + 768 * i, 768), :], weighted[...], preferred_element_type=F32) for i in range(2)]
        for b in range(24):
            for h in range(2):
                for r in range(2):
                    for t in range(2):
                        first = (b % 12) * 64 + h * 32 + r * 16
                        part = got[b // 12][first : first + 16, t * 128 : t * 128 + 128]
                        loads[1 + b, h, r * 2 + t] = part.astype(BF16)
        yield

        @pl.loop(0, 64, unroll=4)
        def _(k):
            ky, kz, kx = k // 16, (k // 4) % 4, k % 4
            j = inv_low[k]
            s_low[c, 0, kx, ky, kz] = loads[j, 0]
            s_low[c, 1, ky, kx, kz] = loads[j, 1]

    def project(c):
        cols = pl.ds(c * 256, 256)
        proj[:, cols] = jnp.dot(turned[pl.ds(2048, 128), :], weighted[...], preferred_element_type=F32).astype(BF16)

    def top_path(c):
        q, p = lines[c][:2]
        m, m_line, m_back = comm.ids(15), comm.ids(7), comm.ids(15)
        s, pt, out, got, g = s_top.at[c], tp.at[c], line_out.at[c], line_in.at[c], gath.at[c]
        offsets = [(dq, dp) for dq in range(4) for dp in range(4) if dq + dp > 0]
        plane = sorted(offsets, key=lambda v: -(min(v[0], 4 - v[0]) + min(v[1], 4 - v[1])))

        def plane_dev(v, w):
            return {"leaf": w * 16 + z * 4 + v} if c == 0 else {"leaf": v * 16 + z * 4 + w}

        comm.recv(m_swap[c], take.at[c], mate_dev)

        @pl.loop(0, 64, unroll=4)
        def _(t):
            i, r, k = t // 16, (t // 2) % 8, t % 2
            one = top_loads[c, inv_top[4 * core + i], r, k]
            two = top_loads[c, inv_top[8 + 4 * core + i], r, k]
            mine = jnp.concatenate([one, two], axis=0) + take[c, t].astype(F32)
            s_top[c, t // 16, (t // 4) % 4, t % 4] = mine.astype(BF16)

        for i, (dq, dp) in enumerate(plane):
            to_q, to_p = (q + dq) % 4, (p + dp) % 4
            comm.send(m[i], s.at[to_q, to_p], pt.at[i], plane_dev(to_q, to_p))
        yield
        total = s_top[c, q, p].astype(F32)
        for i, (dq, dp) in enumerate(plane):
            comm.recv(m[i], pt.at[i], plane_dev((q + dq) % 4, (p + dp) % 4))
            total = total + tp[c, i].astype(F32)
        for h in range(2):
            for k in range(2):
                two = [total[2 * k + i, 8 * h : 8 * h + 8] for i in range(2)]
                line_out[c, h, k] = jnp.concatenate(two, axis=0).astype(BF16)
        for d in (1, 2, 3):
            comm.send(m_line[d - 1], out.at[half], got.at[d - 1], zdev((z + d) % 4))
        for d in range(4):
            comm.send(m_line[3 + d], out.at[1 - half], got.at[3 + d], far_zdev((z + d) % 4))
        yield
        total = line_out[c, half].astype(F32)
        for d in (1, 2, 3):
            comm.recv(m_line[d - 1], got.at[d - 1], zdev((z + d) % 4))
            total = total + line_in[c, d - 1].astype(F32)
        for d in range(4):
            comm.recv(m_line[3 + d], got.at[3 + d], far_zdev((z + d) % 4))
            total = total + line_in[c, 3 + d].astype(F32)
        gath[c, q, p] = total.astype(BF16)
        for i, (dq, dp) in enumerate(plane):
            comm.send(m_back[i], g.at[q, p], g.at[q, p], plane_dev((q + dq) % 4, (p + dp) % 4))
        yield
        for i, (dq, dp) in enumerate(plane):
            comm.recv(m_back[i], g.at[(q + 4 - dq) % 4, (p + 4 - dp) % 4], plane_dev((q + dq) % 4, (p + dp) % 4))
        for t in range(64):
            i, r, k = t // 16, (t // 2) % 8, t % 2
            part = gath[c, t // 16, (t // 4) % 4, (t % 4) // 2].astype(F32)[(t % 2) * 8 : (t % 2) * 8 + 8]
            full_top[i, pl.ds(r * 8, 8), pl.ds(c * 256 + k * 128, 128)] = part

    def scatter(c, h):
        return scatter_steps(
            comm, s_low.at[c, h], r1.at[c, h], r2.at[c, h], rp1.at[c, h], rp2.at[c, h], rz.at[c, h], sums.at[c, h],
            *lines[h],
        )

    m_swap = comm.ids(2)

    work = [compute_steps(0), compute_steps(1)]
    sc = [scatter(0, 0), scatter(0, 1), scatter(1, 0), scatter(1, 1)]
    path = [top_path(0), top_path(1)]

    def run_plan(plan):
        for step in plan:
            if step == "a":
                advance(ga[0], gb[0])
            elif step == "b":
                advance(ga[1], gb[1])
            elif step == "t":
                advance(gt)
            elif step in "vw":
                advance(work["vw".index(step)])
            elif step == "s":
                advance(sc[0], sc[1])
            elif step == "u":
                advance(sc[2], sc[3])
            elif step in "pq":
                advance(path["pq".index(step)])
            elif step in "jk":
                project("jk".index(step))
            elif step == "f":
                fetch[8].wait()
            elif step == "6":
                for i in range(9, len(fetch)):
                    fetch[i].wait()
                turn_modes()
            else:
                turn(int(step))

    run_plan(GATHER_PLAN)
    run_together(ga[0], gb[0], gt)
    run_plan(FIRST_PLAN)
    run_together(work[0], ga[1], gb[1])
    run_plan(SECOND_PLAN)
    run_together(work[1])
    run_plan(LAST_PLAN)
    run_together(path[1], sc[0], sc[1], sc[2], sc[3], path[0])

    for c in range(2):
        for h in range(2):
            for r in range(2):
                for t in range(2):
                    rows, cols = pl.ds(h * 32 + r * 16, 16), pl.ds(c * 256 + t * 128, 128)
                    full_low[rows, cols] = sums[c, h, r * 2 + t]
    comm.finish()


def finish_kernel(full_top, full_low, part, kinv_turned, kinv_low, new_top, new_low, proj):
    proj[...] = part[...]
    new_low[...] = jnp.dot(kinv_low[...], full_low[...], preferred_element_type=F32, precision=lax.Precision.HIGHEST)
    kinv_top = kinv_turned[...].T
    for b in range(4):
        rows = pl.ds(b * 64, 64)
        new_top[rows, :] = jnp.dot(
            kinv_top[b * 64 : b * 64 + 64], full_top[b], preferred_element_type=F32, precision=lax.Precision.HIGHEST
        )


def per_device(top_modes, low_modes, anc_top, anc_low, coupling, leaf_mass, leaf_modes, leaf_coef, kinv_top, kinv_low):
    smem = pl.BlockSpec(memory_space=pltpu.SMEM)
    vmem = pl.BlockSpec(memory_space=pltpu.VMEM)
    hbm = pl.BlockSpec(memory_space=pl.ANY)
    tile, four = (16, 128), (4, 16, 128)
    messages = 4 * 23 + 25 + 4 * 23 + 2 * 37 + 2
    full_top, full_low, part = pl.pallas_call(
        kernel,
        out_shape=(
            jax.ShapeDtypeStruct((4, 64, 512), F32),
            jax.ShapeDtypeStruct((64, 512), F32),
            jax.ShapeDtypeStruct((128, 512), BF16),
        ),
        in_specs=[smem] * 2 + [hbm] * 6,
        out_specs=(vmem, vmem, vmem),
        scratch_shapes=[
            pltpu.VMEM((128, 512), BF16),
            pltpu.VMEM((1536, 2048), BF16),
            pltpu.VMEM((1536, 1536), BF16),
            pltpu.VMEM((1536, 128), BF16),
            pltpu.VMEM((2176, 1536), BF16),
            *([pltpu.VMEM((4, 4, 4, 32, 256), BF16)] * 4),
            pltpu.VMEM((4, 4, 2, 4, 32, 128), BF16),
            pltpu.VMEM((2048, 256), BF16),
            pltpu.VMEM((1536, 256), BF16),
            pltpu.VMEM((1536, 256), BF16),
            pltpu.VMEM((25, 2) + four, BF16),
            pltpu.VMEM((2, 9, 8, 2, 8, 128), F32),
            pltpu.VMEM((2, 64) + tile, BF16),
            pltpu.VMEM((2, 64) + tile, BF16),
            pltpu.VMEM((2, 2, 4, 4, 4) + four, BF16),
            pltpu.VMEM((2, 2, 2, 4, 2) + four, BF16),
            pltpu.VMEM((2, 2, 2, 4, 4) + four, BF16),
            pltpu.VMEM((2, 2, 2, 2) + four, BF16),
            pltpu.VMEM((2, 2, 2, 4) + four, BF16),
            pltpu.VMEM((2, 2, 3) + four, BF16),
            pltpu.VMEM((2, 2) + four, F32),
            pltpu.VMEM((2, 4, 4, 4) + tile, BF16),
            pltpu.VMEM((2, 15, 4) + tile, BF16),
            pltpu.VMEM((2, 2, 2) + tile, BF16),
            pltpu.VMEM((2, 7, 2) + tile, BF16),
            pltpu.VMEM((2, 4, 4, 2) + tile, BF16),
            pltpu.SMEM((16,), jnp.int32),
            pltpu.SMEM((64,), jnp.int32),
            pltpu.SemaphoreType.DMA((12,)),
            pltpu.SemaphoreType.DMA((messages,)),
            pltpu.SemaphoreType.DMA((messages,)),
        ],
        compiler_params=pltpu.CompilerParams(
            collective_id=0, has_side_effects=True, vmem_limit_bytes=63000 * 1024
        ),
    )(
        anc_top[0], anc_low[0],
        top_modes.reshape(4, 2, 32, 512), low_modes.reshape(2, 32, 512), leaf_coef,
        coupling, leaf_mass, leaf_modes,
    )
    return pl.pallas_call(
        finish_kernel,
        out_shape=(
            jax.ShapeDtypeStruct((256, 512), F32),
            jax.ShapeDtypeStruct((64, 512), F32),
            jax.ShapeDtypeStruct((128, 512), BF16),
        ),
        in_specs=[vmem] * 5,
        out_specs=(vmem, vmem, vmem),
    )(full_top, full_low, part, kinv_top.T, kinv_low)


def solution(mesh):
    both = P(("group", "leaf"), None)
    return jax.shard_map(
        per_device,
        mesh=mesh,
        in_specs=(P("group", None), both, both, both, both, both, both, both, P("group", None), both),
        out_specs=(P("group", None), both, both),
        check_vma=False,
    )
```
